32 devices in a mesh: agent: 8 (over y, x, core), res: 4 (over z).
Axes of the slice: x: 2, y: 2, z: 4, core: 2. Of those that a mesh axis runs over, the one named last changes fastest.
Arguments:
- linear_cost: float32 [2048, 2048], P('agent', 'res'), may hold values from -6 to 6
- agent_type: int32 [2048], P('agent'), may hold values from 0 to 3, as said below
- block_mask: int32 [2048, 16], P('agent', 'res'), may hold values 0 or 1
- inverses: bfloat16 [4, 2048, 2048], P(None, 'res'), as said below
- cost_weight: float32 [2048], P('res'), may hold values from 0.5 to 8
- target: float32 [2048], P('res'), may hold values from -6 to 6
Outputs:
- usage: float32 [2048, 2048], P('agent', 'res')
- shared: float32 [2048], P('res')
- prices: float32 [2048], P('res')
- primal_norm: float32 [5], replicated
- dual_norm: float32 [5], replicated
The draws below stay inside these ranges and needn't reach their ends.
Inputs may be any that keep to these rules, and one draw needn't show every extreme that they name: Each inverses[k] is exactly symmetric: inverses[k, i, j] equals inverses[k, j, i]. `agent_type`: each aligned block of 256 agents (the agents held by one device along the agent axis) holds exactly 64 agents of each type, in no particular order.
All inputs are finite; a program needn't handle non-finite values. No bound on the sum of `block_mask` on one device may be relied on, other than what follows from the above.
Results may differ from the reference program's by a relative error of at most 0.0039.
Values may be sent and summed in bfloat16 or wider, within the bound.
No kernel may reach another device: no remote copies, remote signals or barrier semaphores. Data moves between devices by JAX's collectives and lax.ppermute only.
A program may use at most 64 MiB of HBM per device.

```python
import math
import jax
import jax.numpy as jnp
from jax import lax

R = 2048
BLK = 128
TYPES = 4
ITERS = 5
AG_DEV = 256
AGENTS = 2048
NBLK = 16


def draw_agent_type(key, part):
    block_count = AGENTS // AG_DEV
    keys = jax.random.split(jax.random.fold_in(key, 29), block_count)
    base = (jnp.arange(AG_DEV, dtype=jnp.int32) % TYPES).astype(jnp.int32)
    blocks = jax.vmap(lambda single: jax.random.permutation(single, base))(keys)
    return blocks.reshape(AGENTS).astype(jnp.int32)


def draw_inverses(key, part):
    first_key, second_key = jax.random.split(jax.random.fold_in(key, 17), 2)
    gauss = jax.random.normal(first_key, (TYPES, R, R), jnp.float32)
    off_scale = 0.15
    diagonal = jax.random.uniform(second_key, (TYPES, R), jnp.float32, 0.4, 1.0)
    symmetric = (gauss + jnp.swapaxes(gauss, 1, 2)) * (off_scale / jnp.sqrt(2.0 * R))
    identity = jnp.eye(R, dtype=jnp.float32)
    matrix = symmetric * (1.0 - identity) + diagonal[:, :, None] * identity
    return matrix.astype(jnp.bfloat16)


def with_ends(values, rng, low, high):
    longest = values.shape.index(max(values.shape))
    spots = []
    for shift in (0, 1):
        where = [jax.random.randint(jax.random.fold_in(rng, axis), (), 0, length) for axis, length in enumerate(values.shape)]
        where[longest] = (where[longest] + shift) % values.shape[longest]
        spots.append(tuple(where))
    return values.at[spots[0]].set(low).at[spots[1]].set(high)


def level_of(stream_key, extent, cuts, smallest, largest):
    gain, own = 1.0, jax.random.fold_in(stream_key, 6)
    for dim, parts in cuts:
        heights = jnp.exp(jax.random.uniform(jax.random.fold_in(own, dim), (parts,), jnp.float32, smallest / len(cuts), largest / len(cuts)))
        gain = gain * jnp.repeat(heights, extent[dim] // parts).reshape([-1 if axis == dim else 1 for axis in range(len(extent))])
    return gain


def scatter_about(own_key, shape, spread, reach, shards=(), kind=jnp.bfloat16):
    drawn = spread * jax.random.normal(own_key, shape, jnp.float32)
    if shards:
        drawn = drawn * level_of(own_key, shape, shards, -0.22, 0.18)
    return jnp.clip(drawn, -reach, reach).astype(kind)


def setup_inputs(seed: int = 0) -> dict:
    streams_of = jax.random.split(jax.random.key(seed), 7)
    return {
        "linear_cost": scatter_about(streams_of[0], (AGENTS, R), 1.0, 6.0, ((0, 8), (1, 4)), jnp.float32),
        "agent_type": draw_agent_type(jax.random.fold_in(streams_of[6], 71), 0),
        "block_mask": with_ends((jax.random.randint(streams_of[2], (AGENTS, NBLK), 0, 4) < 3).astype(jnp.int32), jax.random.fold_in(streams_of[2], 1), 0, 1),
        "inverses": draw_inverses(jax.random.fold_in(streams_of[6], 71), 0),
        "cost_weight": jnp.clip(jnp.exp(math.log(8.0) - 2.7725887 * jax.random.uniform(streams_of[4], (R,), jnp.float32) ** level_of(streams_of[4], (R,), ((0, 4),), -0.2, 0.2)), 0.5, 8.0),
        "target": scatter_about(streams_of[5], (R,), 1.0, 6.0, ((0, 4),), jnp.float32),
    }


penalty = 1.0
eps = 1e-06

def reference(linear_cost, agent_type, block_mask, inverses, cost_weight, target):
    count = linear_cost.shape[0]
    group_rows = count // TYPES
    order = jnp.argsort(agent_type, stable=True).astype(jnp.int32)
    restore = jnp.argsort(order, stable=True).astype(jnp.int32)
    matrices = inverses.astype(jnp.float32)
    expand = jnp.repeat(block_mask.astype(jnp.float32), BLK, axis=1)
    usage = jnp.zeros(linear_cost.shape, jnp.float32)
    mean_usage = jnp.zeros((R,), jnp.float32)
    shared = jnp.zeros((R,), jnp.float32)
    prices = jnp.zeros((R,), jnp.float32)
    primal_list = []
    dual_list = []
    for iteration in range(ITERS):
        rhs = (penalty * (usage - mean_usage + shared - prices) - linear_cost).astype(jnp.bfloat16)
        grouped = rhs[order].astype(jnp.float32).reshape(TYPES, group_rows, R)
        product = jnp.einsum('tar,trw->taw', grouped, matrices).reshape(count, R)
        new_usage = product[restore] * expand
        dual2 = penalty * penalty * jnp.sum((new_usage - usage) ** 2)
        usage = new_usage
        mean_usage = lax.optimization_barrier(jnp.sum(usage, axis=0)) / count
        shared = (cost_weight * target + penalty * (prices + mean_usage)) / (cost_weight + penalty)
        prices = prices + mean_usage - shared
        primal2 = count * jnp.sum((mean_usage - shared) ** 2)
        primal_list.append(jnp.sqrt(primal2 + eps))
        dual_list.append(jnp.sqrt(dual2 + eps))
    return (usage, shared, prices, jnp.stack(primal_list), jnp.stack(dual_list))
```

```python
import functools

import jax
import jax.numpy as jnp
from jax import lax
from jax.experimental import pallas as pl
from jax.experimental.pallas import tpu as pltpu
from jax.sharding import PartitionSpec as P

ITERS = 5
LANES = 128

penalty = 1.0
eps = 1e-06

VMEM = pl.BlockSpec(memory_space=pltpu.VMEM)
SMEM = pl.BlockSpec(memory_space=pltpu.SMEM)
F32 = jnp.float32
BF16 = jnp.bfloat16


def call(body, out_shape, args, scalars=0, name=None, flops=0, limit=24 << 20, scratch=()):
    moved = sum(a.size * a.dtype.itemsize for a in args)
    return pl.pallas_call(
        body,
        out_shape=out_shape,
        in_specs=[SMEM] * scalars + [VMEM] * (len(args) - scalars),
        out_specs=jax.tree.map(lambda _: VMEM, out_shape),
        scratch_shapes=scratch,
        compiler_params=pltpu.CompilerParams(vmem_limit_bytes=limit),
        cost_estimate=pl.CostEstimate(flops=flops, bytes_accessed=moved, transcendentals=0),
        name=name,
    )(*args)


def shaped(shape, dtype):
    return jax.ShapeDtypeStruct(shape, dtype)


def split(value):
    high = value.astype(BF16)
    return high, (value - high.astype(F32)).astype(BF16)


def three(value):
    high = value.astype(BF16)
    rest = value - high.astype(F32)
    middle = rest.astype(BF16)
    return high, middle, (rest - middle.astype(F32)).astype(BF16)


def prep_kernel(types, cost_ref, kind_ref, mask_ref, high_ref, low_ref, expand_ref, sort_ref):
    agents, width = cost_ref.shape
    blocks = mask_ref.shape[1]
    kind = kind_ref[...]
    row = lax.broadcasted_iota(jnp.int32, (agents, agents), 0)
    column = lax.broadcasted_iota(jnp.int32, (agents, agents), 1)
    earlier = (row < column).astype(F32).astype(BF16)
    type_of = lax.broadcasted_iota(jnp.int32, (16, agents), 0)
    member = (jnp.broadcast_to(kind, (16, agents)) == type_of).astype(F32)
    rank = jnp.dot(member.astype(BF16), earlier, preferred_element_type=F32)
    start = type_of.astype(F32) * (agents // types)
    place = jnp.sum(member * (rank + start), axis=0, keepdims=True)
    sort = (row.astype(F32) == jnp.broadcast_to(place, (agents, agents))).astype(F32).astype(BF16)
    sort_ref[...] = sort
    high, low = split(-cost_ref[...])
    high_ref[...] = jnp.dot(sort, high, preferred_element_type=F32).astype(BF16)
    low_ref[...] = jnp.dot(sort, low, preferred_element_type=F32).astype(BF16)
    mask = jnp.dot(sort, mask_ref[...].astype(F32).astype(BF16), preferred_element_type=F32)
    each = width // blocks
    for block in range(blocks):
        expand_ref[:, block * each:(block + 1) * each] = jnp.broadcast_to(
            mask[:, block:block + 1], (agents, each)
        )


def times(left, m_ref, kind, block):
    width = m_ref.shape[1]
    right = m_ref[kind, :, pl.ds(pl.multiple_of(block * width, LANES), width)]
    return lax.dot_general(left, right, (((1,), (1,)), ((), ())), preferred_element_type=F32)


def first_kernel(slots, me_ref, *refs):
    low_ref, m_ref, acc_ref = refs[slots], refs[slots + 1], refs[slots + 2]
    types = m_ref.shape[0]
    group = low_ref.shape[0] // types
    me = me_ref[0]
    for kind in range(types):
        rows = slice(kind * group, (kind + 1) * group)
        both = jnp.concatenate([refs[0][rows], low_ref[rows]], axis=0)
        own = times(both, m_ref, kind, me)
        total = own[:group] + own[group:]
        for slot in range(1, slots):
            total += times(refs[slot][rows], m_ref, kind, me ^ slot)
        acc_ref[rows] = total


def vectors(received_ref, weight, target, prices, per_block, count):
    width = weight.shape[1]
    parts, changes = [], []
    blocks = weight.shape[0]
    for block in range(blocks):
        rows = received_ref[block * per_block:(block + 1) * per_block]
        parts.append(jnp.sum(rows[:, :width], axis=0, keepdims=True))
        changes.append(jnp.sum(rows[:, width:], axis=0, keepdims=True))
    mean = jnp.concatenate(parts, axis=0) / count
    shared = (weight * target + penalty * (prices + mean)) / (weight + penalty)
    prices = prices + mean - shared
    gap = mean - shared
    primal = count * jnp.sum(gap * gap)
    dual = penalty * penalty * jnp.sum(sum(changes))
    return mean, shared, prices, primal, dual


def norms_of(norms, step, primal, dual):
    lane = lax.broadcasted_iota(jnp.int32, norms.shape, 1)
    row = lax.broadcasted_iota(jnp.int32, norms.shape, 0)
    norms = jnp.where((lane == step) & (row == 0), jnp.sqrt(primal + eps), norms)
    return jnp.where((lane == step) & (row == 1), jnp.sqrt(dual + eps), norms)


def mid_kernel(slots, step, per_block, count, me_ref, *refs):
    usage_ref, received_ref, weight_ref, target_ref, prices_ref, norms_ref, base_ref, m_ref = refs[slots:slots + 8]
    acc_ref, new_prices_ref, new_norms_ref, v_ref = refs[slots + 8:]
    types, width = m_ref.shape[:2]
    blocks = m_ref.shape[2] // width
    group = base_ref.shape[0] // types
    me = me_ref[0]
    mean, shared, prices, primal, dual = vectors(
        received_ref, weight_ref[...], target_ref[...], prices_ref[...], per_block, count
    )
    new_prices_ref[...] = prices
    new_norms_ref[...] = norms_of(norms_ref[...], step, primal, dual)
    v_ref[...] = shared - mean - prices
    row = lax.broadcasted_iota(jnp.int32, (16, width), 0)
    lefts = []
    for slot in range(blocks):
        value = v_ref[pl.ds(me ^ slot, 1), :]
        high, middle, low = (jnp.broadcast_to(x.astype(F32), (16, width)) for x in three(value))
        lefts.append(
            jnp.where(row == 0, high, jnp.where(row == 1, middle, jnp.where(row == 2, low, 0.0))).astype(BF16)
        )
    for kind in range(types):
        rows = slice(kind * group, (kind + 1) * group)
        own_high = refs[0][rows]
        own_low = (usage_ref[rows] - own_high.astype(F32)).astype(BF16)
        own = times(jnp.concatenate([own_high, own_low, lefts[0]], axis=0), m_ref, kind, me)
        total = own[:group] + own[group:2 * group]
        shift = own[2 * group:]
        for slot in range(1, blocks):
            if slot < slots:
                got = times(jnp.concatenate([refs[slot][rows], lefts[slot]], axis=0), m_ref, kind, me ^ slot)
                total += got[:group]
                shift += got[group:]
            else:
                shift += times(lefts[slot], m_ref, kind, me ^ slot)
        acc_ref[rows] = base_ref[rows] + total + jnp.sum(shift, axis=0, keepdims=True)


def late_kernel(first, me_ref, acc_ref, last_ref, expand_ref, usage_ref, m_ref, new_ref, sent_ref, payload_ref, *rest):
    types, width = m_ref.shape[:2]
    blocks = m_ref.shape[2] // width
    group = acc_ref.shape[0] // types
    me = me_ref[0]
    sums = jnp.zeros((8, width), F32)
    change = jnp.zeros((8, width), F32)
    for kind in range(types):
        rows = slice(kind * group, (kind + 1) * group)
        total = acc_ref[rows] + times(last_ref[rows], m_ref, kind, me ^ (blocks - 1))
        if first:
            rest[0][rows] = total
        new = expand_ref[rows] * total
        new_ref[rows] = new
        sent_ref[rows] = new.astype(BF16)
        moved = new if first else new - usage_ref[rows]
        sums += jnp.sum(new.reshape(group // 8, 8, width), axis=0)
        change += jnp.sum((moved * moved).reshape(group // 8, 8, width), axis=0)
    payload_ref[:, :width] = jnp.sum(sums, axis=0, keepdims=True)
    lanes = sum(change[:, at:at + LANES] for at in range(0, width, LANES))
    payload_ref[:, width:] = jnp.sum(lanes, axis=0, keepdims=True)


def last_kernel(step, per_block, count, me_ref, received_ref, weight_ref, target_ref, prices_ref, norms_ref,
                own_shared_ref, own_prices_ref, new_norms_ref, keep_ref):
    mean, shared, prices, primal, dual = vectors(
        received_ref, weight_ref[...], target_ref[...], prices_ref[...], per_block, count
    )
    new_norms_ref[...] = norms_of(norms_ref[...], step, primal, dual)
    keep_ref[...] = shared
    own_shared_ref[...] = keep_ref[pl.ds(me_ref[0], 1), :]
    keep_ref[...] = prices
    own_prices_ref[...] = keep_ref[pl.ds(me_ref[0], 1), :]


def restore_kernel(sort_ref, usage_ref, out_ref):
    total = None
    for piece in three(usage_ref[...]):
        got = lax.dot_general(sort_ref[...], piece, (((0,), (0,)), ((), ())), preferred_element_type=F32)
        total = got if total is None else total + got
    out_ref[...] = total


def on_device(linear_cost, agent_type, block_mask, inverses, cost_weight, target):
    agents, width = linear_cost.shape
    types = inverses.shape[0]
    per_block = lax.axis_size("agent")
    blocks = lax.axis_size("res")
    count = agents * per_block
    me = lax.axis_index("res").astype(jnp.int32).reshape(1)
    flops = 2 * agents * width * width

    def swap(value, bit):
        return lax.ppermute(value, "res", [(i, i ^ bit) for i in range(blocks)])

    def gather(own):
        slots = [own] + [None] * (blocks - 1)
        for slot in sorted(range(1, blocks), key=lambda m: (bin(m).count("1"), -m)):
            bit = slot & -slot
            slots[slot] = swap(slots[slot ^ bit], bit)
        return slots

    def spread(row):
        rows = jnp.broadcast_to(row, (blocks * per_block, row.shape[1]))
        return lax.all_to_all(rows, ("res", "agent"), 0, 0, tiled=True)

    high, low, expand, sort = call(
        functools.partial(prep_kernel, types),
        (shaped((agents, width), BF16), shaped((agents, width), BF16), shaped((agents, width), F32), shaped((agents, agents), BF16)),
        (linear_cost, agent_type.reshape(1, agents), block_mask),
        name="prep",
    )
    slots = gather(high)
    both = spread(jnp.concatenate([cost_weight, target]).reshape(1, 2 * width))[::per_block]
    weights, targets = both[:, :width], both[:, width:]
    prices = jnp.zeros((blocks, width), F32)
    norms = jnp.zeros((8, LANES), F32)
    base = usage = None
    for step in range(ITERS):
        if step == 0:
            acc = call(
                functools.partial(first_kernel, blocks - 1),
                shaped((agents, width), F32),
                (me, *slots[:-1], low, inverses),
                scalars=1, name="first", flops=flops * blocks,
            )
        else:
            acc, prices, norms = call(
                functools.partial(mid_kernel, blocks - 1, step - 1, per_block, count),
                (shaped((agents, width), F32), shaped((blocks, width), F32), shaped((8, LANES), F32)),
                (me, *slots[:-1], usage, received, weights, targets, prices, norms, base, inverses),
                scalars=1, name="mid", flops=flops * blocks,
                scratch=[pltpu.VMEM((blocks, width), F32)],
            )
        outs = (shaped((agents, width), F32), shaped((agents, width), BF16), shaped((1, width + LANES), F32))
        if step == 0:
            outs += (shaped((agents, width), F32),)
        got = call(
            functools.partial(late_kernel, step == 0),
            outs,
            (me, acc, slots[-1], expand, acc if usage is None else usage, inverses),
            scalars=1, name="late", flops=flops,
        )
        usage, sent, payload = got[:3]
        if step == 0:
            base = got[3]
        if step < ITERS - 1:
            slots = gather(sent)
        received = spread(payload)
    own_shared, own_prices, norms = call(
        functools.partial(last_kernel, ITERS - 1, per_block, count),
        (shaped((1, width), F32), shaped((1, width), F32), shaped((8, LANES), F32)),
        (me, received, weights, targets, prices, norms),
        scalars=1, name="last",
        scratch=[pltpu.VMEM((blocks, width), F32)],
    )
    out = call(restore_kernel, shaped((agents, width), F32), (sort, usage), name="restore")
    return out, own_shared.reshape(width), own_prices.reshape(width), norms[0, :ITERS], norms[1, :ITERS]


def solution(mesh):
    placed = (
        P("agent", "res"),
        P("agent"),
        P("agent", "res"),
        P(None, "res", None),
        P("res"),
        P("res"),
    )
    return jax.shard_map(
        on_device,
        mesh=mesh,
        in_specs=placed,
        out_specs=(P("agent", "res"), P("res"), P("res"), P(), P()),
        check_vma=False,
    )
```

```python
import functools

import jax
import jax.numpy as jnp
from jax import lax
from jax.experimental import pallas as pl
from jax.experimental.pallas import tpu as pltpu
from jax.sharding import PartitionSpec as P

ITERS = 5
LANES = 128

penalty = 1.0
eps = 1e-06

VMEM = pl.BlockSpec(memory_space=pltpu.VMEM)
SMEM = pl.BlockSpec(memory_space=pltpu.SMEM)
HBM = pl.BlockSpec(memory_space=pltpu.HBM)
F32 = jnp.float32
BF16 = jnp.bfloat16


def call(body, out_shape, args, scalars=0, far=(), name=None, flops=0, limit=24 << 20, scratch=()):
    moved = sum(a.size * a.dtype.itemsize for a in args)
    args = [pltpu.with_memory_space_constraint(a, pltpu.HBM) if at in far else a for at, a in enumerate(args)]
    spaces = [HBM if at in far else SMEM if at < scalars else VMEM for at in range(len(args))]
    return pl.pallas_call(
        body,
        out_shape=out_shape,
        in_specs=spaces,
        out_specs=jax.tree.map(lambda _: VMEM, out_shape),
        scratch_shapes=scratch,
        compiler_params=pltpu.CompilerParams(vmem_limit_bytes=limit),
        cost_estimate=pl.CostEstimate(flops=flops, bytes_accessed=moved, transcendentals=0),
        name=name,
    )(*args)


def shaped(shape, dtype):
    return jax.ShapeDtypeStruct(shape, dtype)


def split(value):
    high = value.astype(BF16)
    return high, (value - high.astype(F32)).astype(BF16)


def three(value):
    high = value.astype(BF16)
    rest = value - high.astype(F32)
    middle = rest.astype(BF16)
    return high, middle, (rest - middle.astype(F32)).astype(BF16)


def prep_kernel(types, cost_far, kind_far, mask_far, high_ref, low_ref, expand_ref, sort_ref, cost_ref, kind_ref, mask_ref, sems):
    copies = [
        pltpu.make_async_copy(far, near, sems.at[at])
        for at, (far, near) in enumerate(((kind_far, kind_ref), (mask_far, mask_ref), (cost_far, cost_ref)))
    ]
    for copy in copies:
        copy.start()
    agents, width = cost_ref.shape
    blocks = mask_ref.shape[0]
    copies[0].wait()
    kind = kind_ref[...]
    row = lax.broadcasted_iota(jnp.int32, (agents, agents), 0)
    column = lax.broadcasted_iota(jnp.int32, (agents, agents), 1)
    earlier = (row < column).astype(F32).astype(BF16)
    type_of = lax.broadcasted_iota(jnp.int32, (16, agents), 0)
    member = (jnp.broadcast_to(kind, (16, agents)) == type_of).astype(F32)
    rank = jnp.dot(member.astype(BF16), earlier, preferred_element_type=F32)
    start = type_of.astype(F32) * (agents // types)
    place = jnp.sum(member * (rank + start), axis=0, keepdims=True)
    sort = (row.astype(F32) == jnp.broadcast_to(place, (agents, agents))).astype(F32).astype(BF16)
    sort_ref[...] = sort
    copies[2].wait()
    high, low = split(-cost_ref[...])
    high_ref[...] = jnp.dot(sort, high, preferred_element_type=F32).astype(BF16)
    low_ref[...] = jnp.dot(sort, low, preferred_element_type=F32).astype(BF16)
    copies[1].wait()
    mask = lax.dot_general(
        sort, mask_ref[...].astype(F32).astype(BF16), (((1,), (1,)), ((), ())), preferred_element_type=F32
    )
    each = width // blocks
    for block in range(blocks):
        expand_ref[:, block * each:(block + 1) * each] = jnp.broadcast_to(
            mask[:, block:block + 1], (agents, each)
        )


def times(left, right):
    return lax.dot_general(left, right, (((1,), (1,)), ((), ())), preferred_element_type=F32)


def fetch(m_far, m_ref, last_ref, sems, me):
    slots, types, width = m_ref.shape[0] + 1, m_ref.shape[1], m_ref.shape[2]
    copies = {}
    for kind in range(types):
        for slot in range(slots):
            at = pl.multiple_of((me ^ slot) * width, LANES)
            copies[slot, kind] = pltpu.make_async_copy(
                m_far.at[kind, :, pl.ds(at, width)],
                last_ref.at[kind] if slot == slots - 1 else m_ref.at[slot, kind],
                sems.at[slot, kind],
            )
            copies[slot, kind].start()
    return copies


def first_kernel(slots, me_ref, *refs):
    low_ref, m_far, acc_ref, last_ref, m_ref, sems = refs[slots:]
    types = m_ref.shape[1]
    group = low_ref.shape[0] // types
    copies = fetch(m_far, m_ref, last_ref, sems, me_ref[0])
    for kind in range(types):
        rows = slice(kind * group, (kind + 1) * group)
        copies[0, kind].wait()
        own = times(jnp.concatenate([refs[0][rows], low_ref[rows]], axis=0), m_ref[0, kind])
        total = own[:group] + own[group:]
        for slot in range(1, slots):
            copies[slot, kind].wait()
            total += times(refs[slot][rows], m_ref[slot, kind])
        copies[slots, kind].wait()
        acc_ref[rows] = total


def vectors(received_ref, weight, target, prices, per_block, count):
    width = weight.shape[1]
    parts, changes = [], []
    blocks = weight.shape[0]
    for block in range(blocks):
        rows = jnp.sum(received_ref[block * per_block:(block + 1) * per_block], axis=0)
        parts.append(rows[:, :width])
        changes.append(rows[:, width:])
    mean = jnp.concatenate(parts, axis=0) / count
    shared = (weight * target + penalty * (prices + mean)) / (weight + penalty)
    prices = prices + mean - shared
    gap = mean - shared
    primal = count * jnp.sum(gap * gap)
    dual = penalty * penalty * jnp.sum(sum(changes))
    return mean, shared, prices, primal, dual


def norms_of(norms, step, primal, dual):
    lane = lax.broadcasted_iota(jnp.int32, norms.shape, 1)
    row = lax.broadcasted_iota(jnp.int32, norms.shape, 0)
    norms = jnp.where((lane == step) & (row == 0), jnp.sqrt(primal + eps), norms)
    return jnp.where((lane == step) & (row == 1), jnp.sqrt(dual + eps), norms)


def mid_kernel(slots, step, per_block, count, me_ref, *refs):
    usage_ref, received_ref, weight_ref, target_ref, prices_ref, norms_ref, base_ref, m_far = refs[slots:slots + 8]
    acc_ref, new_prices_ref, new_norms_ref, last_ref, v_ref, m_ref, sems = refs[slots + 8:]
    types, width = m_ref.shape[1:3]
    group = base_ref.shape[0] // types
    me = me_ref[0]
    copies = fetch(m_far, m_ref, last_ref, sems, me)
    mean, shared, prices, primal, dual = vectors(
        received_ref, weight_ref[...], target_ref[...], prices_ref[...], per_block, count
    )
    new_prices_ref[...] = prices
    new_norms_ref[...] = norms_of(norms_ref[...], step, primal, dual)
    v_ref[...] = shared - mean - prices
    row = lax.broadcasted_iota(jnp.int32, (16, width), 0)
    lefts = []
    for slot in range(slots + 1):
        value = v_ref[pl.ds(me ^ slot, 1), :]
        high, middle, low = (jnp.broadcast_to(x.astype(F32), (16, width)) for x in three(value))
        lefts.append(
            jnp.where(row == 0, high, jnp.where(row == 1, middle, jnp.where(row == 2, low, 0.0))).astype(BF16)
        )
    for kind in range(types):
        rows = slice(kind * group, (kind + 1) * group)
        own_high = refs[0][rows]
        own_low = (usage_ref[rows] - own_high.astype(F32)).astype(BF16)
        copies[0, kind].wait()
        own = times(jnp.concatenate([own_high, own_low, lefts[0]], axis=0), m_ref[0, kind])
        total = own[:group] + own[group:2 * group]
        shift = own[2 * group:]
        for slot in range(1, slots):
            copies[slot, kind].wait()
            got = times(jnp.concatenate([refs[slot][rows], lefts[slot]], axis=0), m_ref[slot, kind])
            total += got[:group]
            shift += got[group:]
        copies[slots, kind].wait()
        shift += times(lefts[slots], last_ref[kind])
        acc_ref[rows] = base_ref[rows] + total + jnp.sum(shift, axis=0, keepdims=True)


def late_kernel(first, final, acc_ref, slot_ref, expand_ref, usage_ref, last_ref, new_ref, payload_ref, *rest):
    types, width = last_ref.shape[:2]
    group = acc_ref.shape[0] // types
    sums = jnp.zeros((8, width), F32)
    change = jnp.zeros((8, width), F32)
    for kind in range(types):
        rows = slice(kind * group, (kind + 1) * group)
        total = acc_ref[rows] + times(slot_ref[rows], last_ref[kind])
        new = expand_ref[rows] * total
        new_ref[rows] = new
        if not final:
            rest[0][rows] = new.astype(BF16)
        if first:
            rest[1][rows] = total
        moved = new if first else new - usage_ref[rows]
        sums += jnp.sum(new.reshape(group // 8, 8, width), axis=0)
        change += jnp.sum((moved * moved).reshape(group // 8, 8, width), axis=0)
    lanes = sum(change[:, at:at + LANES] for at in range(0, width, LANES))
    row = jnp.concatenate(
        [jnp.sum(sums, axis=0, keepdims=True), jnp.sum(lanes, axis=0, keepdims=True)], axis=1
    )
    payload_ref[...] = jnp.broadcast_to(row[None], payload_ref.shape)


def last_kernel(step, per_block, count, me_ref, received_ref, weight_ref, target_ref, prices_ref, norms_ref,
                own_shared_ref, own_prices_ref, new_norms_ref, keep_ref):
    mean, shared, prices, primal, dual = vectors(
        received_ref, weight_ref[...], target_ref[...], prices_ref[...], per_block, count
    )
    new_norms_ref[...] = norms_of(norms_ref[...], step, primal, dual)
    keep_ref[...] = shared
    own_shared_ref[...] = keep_ref[pl.ds(me_ref[0], 1), :]
    keep_ref[...] = prices
    own_prices_ref[...] = keep_ref[pl.ds(me_ref[0], 1), :]


def restore_kernel(sort_ref, usage_ref, out_ref):
    total = None
    for piece in three(usage_ref[...]):
        got = lax.dot_general(sort_ref[...], piece, (((0,), (0,)), ((), ())), preferred_element_type=F32)
        total = got if total is None else total + got
    out_ref[...] = total


def on_device(linear_cost, agent_type, block_mask, inverses, cost_weight, target):
    agents, width = linear_cost.shape
    types = inverses.shape[0]
    per_block = lax.axis_size("agent")
    blocks = lax.axis_size("res")
    count = agents * per_block
    me = lax.axis_index("res").astype(jnp.int32).reshape(1)
    flops = 2 * agents * width * width

    def swap(value, bit):
        return lax.ppermute(value, "res", [(i, i ^ bit) for i in range(blocks)])

    def gather(own, row):
        slots = [own] + [None] * (blocks - 1)
        order = sorted(range(1, blocks), key=lambda m: (bin(m).count("1"), -m))
        received = None
        for slot in order:
            bit = slot & -slot
            source = slots[slot ^ bit]
            if slot ^ bit and received is None:
                received = spread(row)
                source, received = lax.optimization_barrier((source, received))
            slots[slot] = swap(source, bit)
        return slots, received

    def spread(rows):
        return lax.all_to_all(rows, ("res", "agent"), 0, 0)

    high, low, expand, sort = call(
        functools.partial(prep_kernel, types),
        (shaped((agents, width), BF16), shaped((agents, width), BF16), shaped((agents, width), F32), shaped((agents, agents), BF16)),
        (linear_cost, agent_type.reshape(1, agents), block_mask.T),
        far=(0, 1, 2), name="prep",
        scratch=[
            pltpu.VMEM((agents, width), F32),
            pltpu.VMEM((1, agents), jnp.int32),
            pltpu.VMEM(block_mask.shape[::-1], jnp.int32),
            pltpu.SemaphoreType.DMA((3,)),
        ],
    )
    pair = jnp.concatenate([cost_weight, target]).reshape(1, 1, 2 * width)
    slots, both = gather(high, jnp.broadcast_to(pair, (blocks * per_block, 1, 2 * width)))
    both = both[::per_block, 0]
    weights, targets = both[:, :width], both[:, width:]
    prices = jnp.zeros((blocks, width), F32)
    norms = jnp.zeros((8, LANES), F32)
    matrices = [
        pltpu.VMEM((blocks - 1, types, width, width), BF16),
        pltpu.SemaphoreType.DMA((blocks, types)),
    ]
    last_matrices = shaped((types, width, width), BF16)
    whole = shaped((agents, width), F32)
    base = usage = None
    for step in range(ITERS):
        if step == 0:
            acc, last = call(
                functools.partial(first_kernel, blocks - 1),
                (whole, last_matrices),
                (me, *slots[:-1], low, inverses),
                scalars=1, far=(blocks + 1,), name="first", flops=flops * blocks, scratch=matrices,
            )
        else:
            acc, prices, norms, last = call(
                functools.partial(mid_kernel, blocks - 1, step - 1, per_block, count),
                (whole, shaped((blocks, width), F32), shaped((8, LANES), F32), last_matrices),
                (me, *slots[:-1], usage, received, weights, targets, prices, norms, base, inverses),
                scalars=1, far=(blocks + 7,), name="mid", flops=flops * blocks,
                scratch=[pltpu.VMEM((blocks, width), F32)] + matrices,
            )
        outs = (whole, shaped((blocks * per_block, 1, width + LANES), F32))
        if step < ITERS - 1:
            outs += (shaped((agents, width), BF16),)
        if step == 0:
            outs += (whole,)
        got = call(
            functools.partial(late_kernel, step == 0, step == ITERS - 1),
            outs,
            (acc, slots[-1], expand, acc if usage is None else usage, last),
            name="late", flops=flops,
        )
        usage, payload = got[:2]
        if step == 0:
            base = got[3]
        if step < ITERS - 1:
            slots, received = gather(got[2], payload)
        else:
            received = spread(payload)
    own_shared, own_prices, norms = call(
        functools.partial(last_kernel, ITERS - 1, per_block, count),
        (shaped((1, width), F32), shaped((1, width), F32), shaped((8, LANES), F32)),
        (me, received, weights, targets, prices, norms),
        scalars=1, name="last",
        scratch=[pltpu.VMEM((blocks, width), F32)],
    )
    out = call(restore_kernel, shaped((agents, width), F32), (sort, usage), name="restore")
    return out, own_shared.reshape(width), own_prices.reshape(width), norms[0, :ITERS], norms[1, :ITERS]


def solution(mesh):
    placed = (
        P("agent", "res"),
        P("agent"),
        P("agent", "res"),
        P(None, "res", None),
        P("res"),
        P("res"),
    )
    return jax.shard_map(
        on_device,
        mesh=mesh,
        in_specs=placed,
        out_specs=(P("agent", "res"), P("res"), P("res"), P(), P()),
        check_vma=False,
    )
```
